32 devices in a mesh: group: 4 (over y, core), shard: 8 (over z, x).
Axes of the slice: x: 2, y: 2, z: 4, core: 2. Of those that a mesh axis runs over, the one named last changes fastest.
Arguments:
- queries: bfloat16 [512, 32, 128], P(('group', 'shard')), may hold values from -12 to 12
- passages: bfloat16 [2048, 64, 128], P(('group', 'shard')), may hold values from -4 to 4
- candidates: int32 [512, 160], P(('group', 'shard')), may hold values from 0 to 2047, as said below
- passage_slot: int32 [2048], replicated, may hold values from 0 to 2047, as said below
Outputs:
- scores: float32 [512, 160], P(('group', 'shard'))
The draws below stay inside these ranges and needn't reach their ends.
Inputs may be any that keep to these rules, and one draw needn't show every extreme that they name: `passage_slot`: every storage row is named by exactly one passage id. `candidates`: candidates k * 20 to (k + 1) * 20 - 1 of a query, for k < 8, all lie in the storage rows of one device, rows d * 64 to (d + 1) * 64 - 1 of device d counted group-major. Over the 16 queries of one device, at most 12 such groups name any one device, and some devices are named exactly 12 times by the queries of every device.
All inputs are finite; a program needn't handle non-finite values.
Results may differ from the reference program's by a relative error of at most 0.0003.
Values may be sent and summed in bfloat16 or wider, within the bound.
No kernel may reach another device: no remote copies, remote signals or barrier semaphores. Data moves between devices by JAX's collectives and lax.ppermute only.
A program may use at most 64 MiB of HBM per device.

```python
import jax
import jax.numpy as jnp
from jax import lax

QTOK = 32
PTOK = 64
DIM = 128
PER_VISIT = 20
SPREAD = 8
Q_DEV = 16
SLOT_DEV = 64
PEERS = 32
CAND = 160
VCAP = 12
QUERIES = 512
SLOTS = 2048


def layout(key):
    return jax.random.permutation(jax.random.fold_in(key, 11), SLOTS).astype(jnp.int32)


def entry_scales(key):
    order = jax.random.permutation(jax.random.fold_in(key, 5), DIM).astype(jnp.float32)
    return 2.0 ** (5.0 * order / (DIM - 1) - 2.5)


def draw_queries(key, part):
    scales = entry_scales(key)
    signs = jnp.where(jax.random.bernoulli(jax.random.fold_in(key, 7), 0.5, (QUERIES, QTOK, DIM)), 1.0, -1.0)
    levels = jnp.exp(jax.random.uniform(jax.random.fold_in(key, 9), (QUERIES, QTOK, 1), jnp.float32, jnp.log(0.5), jnp.log(2.0)))
    values = signs * levels / scales[None, None, :]
    return values.astype(jnp.float32).astype(jnp.bfloat16)


def draw_passages(key, part):
    scales = entry_scales(key) * DIM ** (-0.5)
    raw = jax.random.truncated_normal(jax.random.fold_in(key, 13), -3.5, 3.5, (SLOTS, PTOK, DIM), jnp.float32)
    values = raw * scales[None, None, :]
    return values.astype(jnp.float32).astype(jnp.bfloat16)


def draw_passage_slot(key, part):
    return layout(key)


def draw_candidates(key, part):
    placed = layout(key)
    inverse = jnp.zeros((SLOTS,), jnp.int32).at[placed].set(jnp.arange(SLOTS, dtype=jnp.int32))
    device_order = jax.random.permutation(jax.random.fold_in(key, 23), PEERS).astype(jnp.int32)
    device_rank = jnp.zeros((PEERS,), jnp.int32).at[device_order].set(jnp.arange(PEERS, dtype=jnp.int32))
    hot_count = PEERS // 8
    visit_count = Q_DEV * SPREAD
    cold_total = visit_count - hot_count * VCAP
    base_count = cold_total // (PEERS - hot_count)
    extra_count = cold_total % (PEERS - hot_count)
    counts = jnp.where(device_rank < hot_count, VCAP, base_count + (device_rank - hot_count < extra_count).astype(jnp.int32))
    limits = jnp.cumsum(counts.astype(jnp.int32))

    def source(source_index):
        source_key = jax.random.fold_in(key, 1000 + source_index)
        pair_index = jnp.arange(visit_count, dtype=jnp.int32)
        destination = jnp.sum((limits[None, :] <= pair_index[:, None]).astype(jnp.int32), axis=1)
        shuffle = jax.random.permutation(jax.random.fold_in(source_key, 1), visit_count)
        destination = destination[shuffle]
        local_rows = jax.random.randint(jax.random.fold_in(source_key, 2), (visit_count, PER_VISIT), 0, SLOT_DEV)
        storage = destination[:, None] * SLOT_DEV + local_rows
        return inverse[storage].reshape(Q_DEV, SPREAD * PER_VISIT)
    result = jax.vmap(source)(jnp.arange(PEERS, dtype=jnp.int32))
    return result.reshape(QUERIES, CAND).astype(jnp.int32)


def setup_inputs(seed: int = 0) -> dict:
    streams_of = jax.random.split(jax.random.key(seed), 5)
    return {
        "queries": draw_queries(jax.random.fold_in(streams_of[4], 71), 0),
        "passages": draw_passages(jax.random.fold_in(streams_of[4], 71), 0),
        "candidates": draw_candidates(jax.random.fold_in(streams_of[4], 71), 0),
        "passage_slot": draw_passage_slot(jax.random.fold_in(streams_of[4], 71), 0),
    }


def reference(queries, passages, candidates, passage_slot):
    storage = passage_slot[candidates]

    def one_query(pieces):
        query_rows, rows_wanted = pieces
        chosen = passages[rows_wanted].astype(jnp.float32)
        similarity = jnp.einsum("qd,cpd->qcp", query_rows.astype(jnp.float32), chosen)
        return jnp.sum(jnp.max(similarity, axis=2), axis=0) / QTOK

    return lax.map(one_query, (queries, storage))
```

```python
import functools

import jax
import jax.numpy as jnp
from jax import lax
from jax.experimental import pallas as pl
from jax.experimental.pallas import tpu as pltpu
from jax.sharding import PartitionSpec as P

PER_VISIT = 20
LANES = 128
GROUP = 8
SETS = 4
AXES = ("group", "shard")


def lookup(tables, high, low):
    result = jnp.zeros(high.shape, tables[0].dtype)
    for row, table in enumerate(tables):
        picked = jnp.take_along_axis(table, low, axis=1, mode="promise_in_bounds")
        result = jnp.where(high == row, picked, result)
    return result


def prepare_kernel(shape, where_ref, query_ref, cand_ref, slot_ref, block_ref, pick_ref):
    shard_count, z_count, slot_dev, spread = shape
    query_count, qtok, dim = query_ref.shape
    cand_count = cand_ref.shape[1]
    width = pick_ref.shape[1]
    my_core = where_ref[0]
    my_x = where_ref[1]
    cand = cand_ref[...]
    cand = jnp.concatenate(
        [cand, jnp.zeros((query_count, width - cand_count), jnp.int32)], axis=1
    )
    tables = [
        jnp.broadcast_to(slot_ref[row : row + 1, :], (query_count, LANES))
        for row in range(slot_ref.shape[0])
    ]
    parts = []
    for part in range(width // LANES):
        ids = cand[:, part * LANES : (part + 1) * LANES]
        parts.append(lookup(tables, lax.div(ids, LANES), lax.rem(ids, LANES)))
    storage = jnp.concatenate(parts, axis=1)
    device = lax.div(storage, slot_dev)
    group = lax.div(device, shard_count)
    shard = lax.rem(device, shard_count)
    cell = lax.div(group, 2) * z_count + lax.div(shard, 2)
    code = (
        cell * SETS
        + jnp.bitwise_xor(lax.rem(group, 2), my_core) * 2
        + jnp.bitwise_xor(lax.rem(shard, 2), my_x)
    )
    pick_ref[...] = code * slot_dev + lax.rem(storage, slot_dev)
    lane = lax.broadcasted_iota(jnp.int32, (query_count, LANES), 1)
    named = jnp.zeros((query_count, LANES), jnp.float32)
    for visit in range(spread):
        first = visit * PER_VISIT
        hit = code[:, first : first + 1] == lane
        named = jnp.where(hit, 1.0, named)
    rows = query_count * qtok
    block_ref[0:rows, :] = query_ref[...].reshape(rows, dim)
    block_ref[rows : rows + query_count, :] = named.astype(jnp.bfloat16)


def prepare(where, queries, candidates, passage_slot, shape):
    query_count, qtok, dim = queries.shape
    width = -(-candidates.shape[1] // LANES) * LANES
    vmem = pl.BlockSpec(memory_space=pltpu.VMEM)
    return pl.pallas_call(
        functools.partial(prepare_kernel, shape),
        out_shape=(
            jax.ShapeDtypeStruct((query_count * (qtok + 1), dim), jnp.bfloat16),
            jax.ShapeDtypeStruct((query_count, width), jnp.int32),
        ),
        in_specs=[pl.BlockSpec(memory_space=pltpu.SMEM), vmem, vmem, vmem],
        out_specs=(vmem, vmem),
        name="prepare",
    )(where, queries, candidates, passage_slot.reshape(-1, LANES))


def score_kernel(plan, *refs):
    sources, set_ids, n_arrays, n_stores, has_carry, qtok, cells = plan
    where_ref = refs[0]
    arrays = refs[1 : 1 + n_arrays]
    stores = refs[1 + n_arrays : 1 + n_arrays + n_stores]
    rest = refs[1 + n_arrays + n_stores :]
    if has_carry:
        rest = rest[1:]
    (out_ref, qs, ps, mask_v, mask_s, todo, setof, best, copy_sem) = rest
    ptok = stores[0].shape[1]
    slots = stores[0].shape[0]
    dim = stores[0].shape[2]
    query_count = qs.shape[1] // (qtok + 1)
    rows = query_count * qtok
    me = where_ref[2]
    source_count = len(sources)

    q_copies = []
    for position, (array, index) in enumerate(sources):
        source = arrays[array] if index is None else arrays[array].at[index]
        q_copies.append(pltpu.make_async_copy(source, qs.at[position], copy_sem.at[0]))
    p_copies = [
        pltpu.make_async_copy(store, ps.at[position], copy_sem.at[1])
        for position, store in enumerate(stores)
    ]
    for copy in q_copies:
        copy.start()
    for copy in p_copies:
        copy.start()
    for copy in q_copies:
        copy.wait()

    weight = lax.shift_left(1, lax.broadcasted_iota(jnp.int32, (query_count, LANES), 0))
    weight = weight.astype(jnp.float32)
    for position in range(source_count):
        named = qs[position, rows : rows + query_count, :].astype(jnp.float32)
        mask_v[position : position + 1, :] = jnp.sum(
            named * weight, axis=0, keepdims=True
        ).astype(jnp.int32)
    mask_copy = pltpu.make_async_copy(mask_v, mask_s, copy_sem.at[2])
    mask_copy.start()
    mask_copy.wait()

    total = jnp.int32(0)
    for position, set_id in enumerate(set_ids):
        start = total

        def one_source(source, filled):
            bits = mask_s[source, me * SETS + set_id]
            for query in range(query_count):
                todo[filled] = source * query_count + query
                filled = filled + (lax.shift_right_logical(bits, query) & 1)
            return filled

        filled = lax.fori_loop(0, source_count, one_source, start)
        last = todo[jnp.maximum(filled - 1, 0)]
        for extra in range(GROUP - 1):
            todo[filled + extra] = last
        total = lax.div(filled + (GROUP - 1), GROUP) * GROUP

        def mark(group, carry, position=position):
            setof[group] = position
            return carry

        lax.fori_loop(lax.div(start, GROUP), lax.div(total, GROUP), mark, 0)
    groups = lax.div(total, GROUP)

    for copy in p_copies:
        copy.wait()

    columns = GROUP * qtok
    adder = jnp.where(
        lax.div(lax.broadcasted_iota(jnp.int32, (GROUP, columns), 1), qtok)
        == lax.broadcasted_iota(jnp.int32, (GROUP, columns), 0),
        1.0,
        0.0,
    ).astype(jnp.bfloat16)
    contract_last = (((1,), (1,)), ((), ()))
    quarter = lax.div(lax.broadcasted_iota(jnp.int32, (1, SETS * slots), 1), slots)

    def finish(group):
        value = best[...]
        high = value.astype(jnp.bfloat16)
        low = (value - high.astype(jnp.float32)).astype(jnp.bfloat16)
        score = lax.dot_general(adder, high, contract_last, preferred_element_type=jnp.float32)
        score += lax.dot_general(adder, low, contract_last, preferred_element_type=jnp.float32)
        score = score * (1.0 / qtok)
        score = jnp.concatenate([score] * SETS, axis=1)
        position = setof[group]
        set_id = jnp.int32(set_ids[0])
        for other in range(1, len(set_ids)):
            set_id = jnp.where(position == other, set_ids[other], set_id)
        for item in range(GROUP):
            entry = todo[group * GROUP + item]
            source = lax.div(entry, query_count)
            row = where_ref[3 + sources_base(plan) + source] * query_count + lax.rem(
                entry, query_count
            )
            out_ref[pl.ds(row, 1), :] = jnp.where(
                quarter == set_id, score[item : item + 1], out_ref[pl.ds(row, 1), :]
            )

    def search(group):
        pieces = []
        for item in range(GROUP):
            entry = todo[group * GROUP + item]
            source = lax.div(entry, query_count)
            first = pl.multiple_of(lax.rem(entry, query_count) * qtok, qtok)
            pieces.append(qs[source, pl.ds(first, qtok), :])
        query = jnp.concatenate(pieces, axis=0)
        position = setof[group]
        step = 8
        for first in range(0, slots, step):
            tokens = ps[position, first : first + step].reshape(step * ptok, dim)
            similarity = lax.dot_general(
                tokens, query, contract_last, preferred_element_type=jnp.float32
            )
            similarity = similarity.reshape(step, ptok // 8, 8, columns)
            top = similarity[:, 0]
            for other in range(1, ptok // 8):
                top = jnp.maximum(top, similarity[:, other])
            best[first : first + step, :] = jnp.max(top, axis=1)

    @pl.when(groups > 0)
    def _():
        search(0)

        @pl.loop(1, groups)
        def _(group):
            finish(group - 1)
            search(group)

        finish(groups - 1)


def sources_base(plan):
    return 0


def score(where, arrays, sources, stores, set_ids, qtok, cells, carry, name):
    slots, ptok, dim = stores[0].shape
    block_rows = arrays[0].shape[-2]
    query_count = block_rows // (qtok + 1)
    source_count = len(sources)
    mask_rows = -(-source_count // 8) * 8
    entries = len(set_ids) * (source_count * query_count + GROUP) + 2 * GROUP
    plan = (
        tuple(sources),
        tuple(set_ids),
        len(arrays),
        len(stores),
        carry is not None,
        qtok,
        cells,
    )
    operands = [where, *arrays, *stores]
    aliases = {}
    specs = [pl.BlockSpec(memory_space=pltpu.SMEM)]
    specs += [pl.BlockSpec(memory_space=pl.ANY)] * (len(arrays) + len(stores))
    if carry is not None:
        aliases = {len(operands): 0}
        operands.append(carry)
        specs.append(pl.BlockSpec(memory_space=pltpu.VMEM))
    work = len(sources) * query_count * len(stores) // 3
    return pl.pallas_call(
        functools.partial(score_kernel, plan),
        out_shape=jax.ShapeDtypeStruct((cells * query_count, SETS * slots), jnp.float32),
        in_specs=specs,
        out_specs=pl.BlockSpec(memory_space=pltpu.VMEM),
        scratch_shapes=[
            pltpu.VMEM((source_count, block_rows, dim), jnp.bfloat16),
            pltpu.VMEM((len(stores), slots, ptok, dim), jnp.bfloat16),
            pltpu.VMEM((mask_rows, LANES), jnp.int32),
            pltpu.SMEM((mask_rows, LANES), jnp.int32),
            pltpu.SMEM((entries,), jnp.int32),
            pltpu.SMEM((entries // GROUP + 1,), jnp.int32),
            pltpu.VMEM((slots, GROUP * qtok), jnp.float32),
            pltpu.SemaphoreType.DMA((3,)),
        ],
        input_output_aliases=aliases,
        compiler_params=pltpu.CompilerParams(vmem_limit_bytes=48 << 20),
        cost_estimate=pl.CostEstimate(
            flops=2 * work * slots * ptok * qtok * dim * 2,
            bytes_accessed=source_count * block_rows * dim * 2
            + len(stores) * slots * ptok * dim * 2,
            transcendentals=0,
        ),
        name=name,
    )(*operands)


def select_kernel(scores_ref, pick_ref, out_ref):
    cells, query_count, wide = scores_ref.shape
    cand_count = out_ref.shape[1]
    tables = [
        scores_ref[cell, :, part * LANES : (part + 1) * LANES]
        for cell in range(cells)
        for part in range(wide // LANES)
    ]
    parts = []
    for part in range(pick_ref.shape[1] // LANES):
        pick = pick_ref[:, part * LANES : (part + 1) * LANES]
        parts.append(lookup(tables, lax.div(pick, LANES), lax.rem(pick, LANES)))
    out_ref[...] = jnp.concatenate(parts, axis=1)[:, :cand_count]


def select(scores, pick, cand_count):
    vmem = pl.BlockSpec(memory_space=pltpu.VMEM)
    return pl.pallas_call(
        select_kernel,
        out_shape=jax.ShapeDtypeStruct((pick.shape[0], cand_count), jnp.float32),
        in_specs=[vmem, vmem],
        out_specs=vmem,
        name="select",
    )(scores, pick)


def local(mesh_shape, queries, passages, candidates, passage_slot):
    group_count, shard_count = mesh_shape
    y_count, z_count = group_count // 2, shard_count // 2
    cells = y_count * z_count
    query_count, qtok, dim = queries.shape
    slots = passages.shape[0]
    spread = candidates.shape[1] // PER_VISIT

    def index(yh, c, zh, x):
        return (yh * 2 + c) * shard_count + zh * 2 + x

    every = [
        (yh, c, zh, x)
        for yh in range(y_count)
        for c in range(2)
        for zh in range(z_count)
        for x in range(2)
    ]

    def move(value, to):
        pairs = [(index(*device), index(*to(*device))) for device in every]
        return lax.ppermute(value, AXES, pairs)

    group = lax.axis_index("group")
    shard = lax.axis_index("shard")
    my_y, my_core = group // 2, group % 2
    my_z, my_x = shard // 2, shard % 2
    lines = [
        [((my_y - ky) % y_count) * z_count + (my_z - kz) % z_count for kz in range(z_count)]
        for ky in range(y_count)
    ]
    me = my_y * z_count + my_z
    where = jnp.stack(
        [my_core, my_x, me] + [cell for line in lines for cell in line]
    ).astype(jnp.int32)

    store_x = move(passages, lambda yh, c, zh, x: (yh, c, zh, 1 - x))
    store_c = move(passages, lambda yh, c, zh, x: (yh, 1 - c, zh, x))
    block, pick = prepare(
        where, queries, candidates, passage_slot, (shard_count, z_count, slots, spread)
    )
    along_z = [
        move(block, lambda yh, c, zh, x, kz=kz: (yh, c, (zh + kz) % z_count, x))
        for kz in range(1, z_count)
    ]
    near_y = [
        move(block, lambda yh, c, zh, x, ky=ky: ((yh + ky) % y_count, c, zh, x))
        for ky in range(1, y_count)
    ]
    far = jnp.stack(along_z)
    far_y = [
        move(far, lambda yh, c, zh, x, ky=ky: ((yh + ky) % y_count, c, zh, x))
        for ky in range(1, y_count)
    ]
    store_xc = move(store_x, lambda yh, c, zh, x: (yh, 1 - c, zh, x))

    arrays = [block] + along_z
    sources = [(position, None) for position in range(z_count)]
    first = score(
        where, arrays, sources, [passages, store_c], [0, 2], qtok, cells, None, "score_line"
    )
    for near, far_block in zip(near_y, far_y):
        base = len(arrays)
        arrays = arrays + [near, far_block]
        sources = sources + [(base, None)] + [
            (base + 1, kz) for kz in range(z_count - 1)
        ]
    del first
    everything = score(
        where,
        arrays,
        sources,
        [passages, store_x, store_c, store_xc],
        [0, 1, 2, 3],
        qtok,
        cells,
        None,
        "score_all",
    )
    returned = everything.reshape(cells, query_count, SETS * slots)
    members = [
        [index(yh, c, zh, x) for yh in range(y_count) for zh in range(z_count)]
        for c in range(2)
        for x in range(2)
    ]
    returned = lax.all_to_all(
        returned, AXES, 0, 0, tiled=True, axis_index_groups=members
    )
    return select(returned, pick, candidates.shape[1])


def solution(mesh):
    mesh_shape = (mesh.shape["group"], mesh.shape["shard"])
    return jax.shard_map(
        functools.partial(local, mesh_shape),
        mesh=mesh,
        in_specs=(
            P(AXES, None, None),
            P(AXES, None, None),
            P(AXES, None),
            P(),
        ),
        out_specs=P(AXES, None),
        check_vma=False,
    )
```

```python
import functools

import jax
import jax.numpy as jnp
from jax import lax
from jax.experimental import pallas as pl
from jax.experimental.pallas import tpu as pltpu
from jax.sharding import PartitionSpec as P

PER_VISIT = 20
LANES = 128
GROUP = 8
SETS = 4
AXES = ("group", "shard")


def lookup(tables, high, low):
    result = jnp.zeros(high.shape, tables[0].dtype)
    for row, table in enumerate(tables):
        picked = jnp.take_along_axis(table, low, axis=1, mode="promise_in_bounds")
        result = jnp.where(high == row, picked, result)
    return result


def prepare_kernel(shape, where_ref, query_ref, cand_ref, slot_ref, block_ref, pick_ref):
    shard_count, z_count, slot_dev, spread = shape
    query_count, qtok, dim = query_ref.shape
    cand_count = cand_ref.shape[1]
    width = pick_ref.shape[1]
    my_core = lax.rem(lax.div(where_ref[0], shard_count), 2)
    my_x = lax.rem(where_ref[0], 2)
    cand = cand_ref[...]
    cand = jnp.concatenate(
        [cand, jnp.zeros((query_count, width - cand_count), jnp.int32)], axis=1
    )
    tables = [
        jnp.broadcast_to(slot_ref[row : row + 1, :], (query_count, LANES))
        for row in range(slot_ref.shape[0])
    ]
    parts = []
    for part in range(width // LANES):
        ids = cand[:, part * LANES : (part + 1) * LANES]
        parts.append(lookup(tables, lax.div(ids, LANES), lax.rem(ids, LANES)))
    storage = jnp.concatenate(parts, axis=1)
    device = lax.div(storage, slot_dev)
    group = lax.div(device, shard_count)
    shard = lax.rem(device, shard_count)
    cell = lax.div(group, 2) * z_count + lax.div(shard, 2)
    code = (
        cell * SETS
        + jnp.bitwise_xor(lax.rem(group, 2), my_core) * 2
        + jnp.bitwise_xor(lax.rem(shard, 2), my_x)
    )
    pick_ref[...] = code * slot_dev + lax.rem(storage, slot_dev)
    lane = lax.broadcasted_iota(jnp.int32, (query_count, LANES), 1)
    named = jnp.zeros((query_count, LANES), jnp.float32)
    for visit in range(spread):
        first = visit * PER_VISIT
        hit = code[:, first : first + 1] == lane
        named = jnp.where(hit, 1.0, named)
    rows = query_count * qtok
    block_ref[0:rows, :] = query_ref[...].reshape(rows, dim)
    block_ref[rows : rows + query_count, :] = named.astype(jnp.bfloat16)


def prepare(where, queries, candidates, passage_slot, shape):
    query_count, qtok, dim = queries.shape
    width = -(-candidates.shape[1] // LANES) * LANES
    vmem = pl.BlockSpec(memory_space=pltpu.VMEM)
    return pl.pallas_call(
        functools.partial(prepare_kernel, shape),
        out_shape=(
            jax.ShapeDtypeStruct((query_count * (qtok + 1), dim), jnp.bfloat16),
            jax.ShapeDtypeStruct((query_count, width), jnp.int32),
        ),
        in_specs=[pl.BlockSpec(memory_space=pltpu.SMEM), vmem, vmem, vmem],
        out_specs=(vmem, vmem),
        name="prepare",
    )(where, queries, candidates, passage_slot.reshape(-1, LANES))


def score_kernel(plan, *refs):
    arrays_at, set_from, n_arrays, n_stores, has_carry, qtok, y_count, z_count = plan
    where_ref = refs[0]
    arrays = refs[1 : 1 + n_arrays]
    stores = refs[1 + n_arrays : 1 + n_arrays + n_stores]
    rest = refs[1 + n_arrays + n_stores :]
    if has_carry:
        rest = rest[1:]
    (out_ref, qs, ps, mask_v, mask_s, todo, setof, best, copy_sem) = rest
    slots, ptok, dim = stores[0].shape
    query_count = qs.shape[1] // (qtok + 1)
    rows = query_count * qtok
    source_count = len(arrays_at)
    my_y = lax.div(where_ref[0], 4 * z_count)
    my_z = lax.rem(lax.div(where_ref[0], 2), z_count)
    me = my_y * z_count + my_z

    q_copies = []
    for position, (array, index) in enumerate(arrays_at):
        source = arrays[array] if index is None else arrays[array].at[index]
        q_copies.append(pltpu.make_async_copy(source, qs.at[position], copy_sem.at[0]))
    p_copies = [
        pltpu.make_async_copy(store, ps.at[position], copy_sem.at[1])
        for position, store in enumerate(stores)
    ]
    for copy in q_copies:
        copy.start()
    for copy in p_copies:
        copy.start()
    for copy in q_copies:
        copy.wait()

    weight = lax.shift_left(1, lax.broadcasted_iota(jnp.int32, (query_count, LANES), 0))
    weight = weight.astype(jnp.float32)
    for position in range(source_count):
        named = qs[position, rows : rows + query_count, :].astype(jnp.float32)
        mask_v[position : position + 1, :] = jnp.sum(
            named * weight, axis=0, keepdims=True
        ).astype(jnp.int32)
    mask_copy = pltpu.make_async_copy(mask_v, mask_s, copy_sem.at[2])
    mask_copy.start()
    mask_copy.wait()

    total = jnp.int32(0)
    for position, (set_id, from_source) in enumerate(set_from):
        start = total

        def one_source(source, filled, set_id=set_id):
            bits = mask_s[source, me * SETS + set_id]
            for query in range(query_count):
                todo[filled] = source * query_count + query
                filled = filled + (lax.shift_right_logical(bits, query) & 1)
            return filled

        filled = lax.fori_loop(from_source, source_count, one_source, start)
        last = todo[jnp.maximum(filled - 1, 0)]
        for extra in range(GROUP - 1):
            todo[filled + extra] = last
        total = lax.div(filled + (GROUP - 1), GROUP) * GROUP

        def mark(group, carry, position=position):
            setof[group] = position
            return carry

        lax.fori_loop(lax.div(start, GROUP), lax.div(total, GROUP), mark, 0)
    groups = lax.div(total, GROUP)

    for copy in p_copies:
        copy.wait()

    columns = GROUP * qtok
    adder = jnp.where(
        lax.div(lax.broadcasted_iota(jnp.int32, (GROUP, columns), 1), qtok)
        == lax.broadcasted_iota(jnp.int32, (GROUP, columns), 0),
        1.0,
        0.0,
    ).astype(jnp.bfloat16)
    contract_last = (((1,), (1,)), ((), ()))
    quarter = lax.div(lax.broadcasted_iota(jnp.int32, (1, SETS * slots), 1), slots)

    def finish(group):
        value = best[...]
        high = value.astype(jnp.bfloat16)
        low = (value - high.astype(jnp.float32)).astype(jnp.bfloat16)
        score = lax.dot_general(adder, high, contract_last, preferred_element_type=jnp.float32)
        score += lax.dot_general(adder, low, contract_last, preferred_element_type=jnp.float32)
        score = score * (1.0 / qtok)
        score = jnp.concatenate([score] * SETS, axis=1)
        position = setof[group]
        set_id = jnp.int32(set_from[0][0])
        for other in range(1, len(set_from)):
            set_id = jnp.where(position == other, set_from[other][0], set_id)
        for item in range(GROUP):
            entry = todo[group * GROUP + item]
            source = lax.div(entry, query_count)
            from_y = lax.rem(my_y - lax.div(source, z_count) + y_count, y_count)
            from_z = lax.rem(my_z - lax.rem(source, z_count) + z_count, z_count)
            row = (from_y * z_count + from_z) * query_count + lax.rem(entry, query_count)
            out_ref[pl.ds(row, 1), :] = jnp.where(
                quarter == set_id, score[item : item + 1], out_ref[pl.ds(row, 1), :]
            )

    def search(group):
        pieces = []
        for item in range(GROUP):
            entry = todo[group * GROUP + item]
            source = lax.div(entry, query_count)
            first = pl.multiple_of(lax.rem(entry, query_count) * qtok, qtok)
            pieces.append(qs[source, pl.ds(first, qtok), :])
        query = jnp.concatenate(pieces, axis=0)
        position = setof[group]
        step = 8
        for first in range(0, slots, step):
            tokens = ps[position, first : first + step].reshape(step * ptok, dim)
            similarity = lax.dot_general(
                tokens, query, contract_last, preferred_element_type=jnp.float32
            )
            similarity = similarity.reshape(step, ptok // 8, 8, columns)
            top = similarity[:, 0]
            for other in range(1, ptok // 8):
                top = jnp.maximum(top, similarity[:, other])
            best[first : first + step, :] = jnp.max(top, axis=1)

    @pl.when(groups > 0)
    def _():
        search(0)

        @pl.loop(1, groups)
        def _(group):
            finish(group - 1)
            search(group)

        finish(groups - 1)


def score(where, arrays, arrays_at, stores, set_from, qtok, counts, carry):
    slots, ptok, dim = stores[0].shape
    block_rows = arrays[0].shape[-2]
    query_count = block_rows // (qtok + 1)
    source_count = len(arrays_at)
    cells = counts[0] * counts[1]
    mask_rows = -(-source_count // 8) * 8
    entries = len(set_from) * (source_count * query_count + GROUP) + 2 * GROUP
    plan = (
        tuple(arrays_at),
        tuple(set_from),
        len(arrays),
        len(stores),
        carry is not None,
        qtok,
        *counts,
    )
    operands = [where, *arrays, *stores]
    aliases = {}
    specs = [pl.BlockSpec(memory_space=pltpu.SMEM)]
    specs += [pl.BlockSpec(memory_space=pl.ANY)] * (len(arrays) + len(stores))
    if carry is not None:
        aliases = {len(operands): 0}
        operands.append(carry)
        specs.append(pl.BlockSpec(memory_space=pltpu.VMEM))
    work = sum(source_count - from_source for _, from_source in set_from) * query_count // 4
    return pl.pallas_call(
        functools.partial(score_kernel, plan),
        out_shape=jax.ShapeDtypeStruct((cells * query_count, SETS * slots), jnp.float32),
        in_specs=specs,
        out_specs=pl.BlockSpec(memory_space=pltpu.VMEM),
        scratch_shapes=[
            pltpu.VMEM((source_count, block_rows, dim), jnp.bfloat16),
            pltpu.VMEM((len(stores), slots, ptok, dim), jnp.bfloat16),
            pltpu.VMEM((mask_rows, LANES), jnp.int32),
            pltpu.SMEM((mask_rows, LANES), jnp.int32),
            pltpu.SMEM((entries,), jnp.int32),
            pltpu.SMEM((entries // GROUP + 1,), jnp.int32),
            pltpu.VMEM((slots, GROUP * qtok), jnp.float32),
            pltpu.SemaphoreType.DMA((3,)),
        ],
        input_output_aliases=aliases,
        compiler_params=pltpu.CompilerParams(vmem_limit_bytes=48 << 20),
        cost_estimate=pl.CostEstimate(
            flops=4 * work * slots * ptok * qtok * dim,
            bytes_accessed=source_count * block_rows * dim * 2
            + len(stores) * slots * ptok * dim * 2,
            transcendentals=0,
        ),
    )(*operands)


def select_kernel(scores_ref, pick_ref, out_ref):
    cells, _, wide = scores_ref.shape
    cand_count = out_ref.shape[1]
    tables = [
        scores_ref[cell, :, part * LANES : (part + 1) * LANES]
        for cell in range(cells)
        for part in range(wide // LANES)
    ]
    parts = []
    for part in range(pick_ref.shape[1] // LANES):
        pick = pick_ref[:, part * LANES : (part + 1) * LANES]
        parts.append(lookup(tables, lax.div(pick, LANES), lax.rem(pick, LANES)))
    out_ref[...] = jnp.concatenate(parts, axis=1)[:, :cand_count]


def select(scores, pick, cand_count):
    vmem = pl.BlockSpec(memory_space=pltpu.VMEM)
    return pl.pallas_call(
        select_kernel,
        out_shape=jax.ShapeDtypeStruct((pick.shape[0], cand_count), jnp.float32),
        in_specs=[vmem, vmem],
        out_specs=vmem,
        name="select",
    )(scores, pick)


def local(mesh_shape, queries, passages, candidates, passage_slot):
    group_count, shard_count = mesh_shape
    y_count, z_count = group_count // 2, shard_count // 2
    cells = y_count * z_count
    query_count, qtok, _ = queries.shape
    slots = passages.shape[0]
    spread = candidates.shape[1] // PER_VISIT

    def index(yh, c, zh, x):
        return (yh * 2 + c) * shard_count + zh * 2 + x

    every = [
        (yh, c, zh, x)
        for yh in range(y_count)
        for c in range(2)
        for zh in range(z_count)
        for x in range(2)
    ]

    def move(value, to):
        pairs = [(index(*device), index(*to(*device))) for device in every]
        return lax.ppermute(value, AXES, pairs)

    group = lax.axis_index("group")
    shard = lax.axis_index("shard")
    where = (group * shard_count + shard).reshape(1).astype(jnp.int32)

    store_x = move(passages, lambda yh, c, zh, x: (yh, c, zh, 1 - x))
    store_c = move(passages, lambda yh, c, zh, x: (yh, 1 - c, zh, x))
    block, pick = prepare(
        where, queries, candidates, passage_slot, (shard_count, z_count, slots, spread)
    )
    line = [block] + [
        move(block, lambda yh, c, zh, x, kz=kz: (yh, c, (zh + kz) % z_count, x))
        for kz in range(1, z_count)
    ]
    blocks = list(line)
    for ky in range(1, y_count):
        blocks += [
            move(part, lambda yh, c, zh, x, ky=ky: ((yh + ky) % y_count, c, zh, x))
            for part in line
        ]
    at = [(position, None) for position in range(cells)]
    counts = (y_count, z_count)
    own = score(
        where, line, at[:z_count], [passages, store_c], [(0, 0), (2, 0)], qtok, counts, None
    )
    store_x, own = lax.optimization_barrier((store_x, own))
    store_xc = move(store_x, lambda yh, c, zh, x: (yh, 1 - c, zh, x))
    everything = score(
        where,
        blocks,
        at,
        [passages, store_c, store_x, store_xc],
        [(0, z_count), (2, z_count), (1, 0), (3, 0)],
        qtok,
        counts,
        own,
    )
    returned = everything.reshape(cells, query_count, SETS * slots)
    members = [
        [index(yh, c, zh, x) for yh in range(y_count) for zh in range(z_count)]
        for c in range(2)
        for x in range(2)
    ]
    returned = lax.all_to_all(
        returned, AXES, 0, 0, tiled=True, axis_index_groups=members
    )
    return select(returned, pick, candidates.shape[1])


def solution(mesh):
    mesh_shape = (mesh.shape["group"], mesh.shape["shard"])
    return jax.shard_map(
        functools.partial(local, mesh_shape),
        mesh=mesh,
        in_specs=(
            P(AXES, None, None),
            P(AXES, None, None),
            P(AXES, None),
            P(),
        ),
        out_specs=P(AXES, None),
        check_vma=False,
    )
```

```python
import functools

import jax
import jax.numpy as jnp
from jax import lax
from jax.experimental import pallas as pl
from jax.experimental.pallas import tpu as pltpu
from jax.sharding import PartitionSpec as P

PER_VISIT = 20
LANES = 128
GROUP = 8
SETS = 4
AXES = ("group", "shard")


def lookup(tables, high, low):
    result = jnp.zeros(high.shape, tables[0].dtype)
    for row, table in enumerate(tables):
        picked = jnp.take_along_axis(table, low, axis=1, mode="promise_in_bounds")
        result = jnp.where(high == row, picked, result)
    return result


def prepare_kernel(
    shape, where_ref, query_ref, cand_ref, slot_ref, store_ref, block_ref, pick_ref, near_ref, sem
):
    near_copy = pltpu.make_async_copy(store_ref, near_ref, sem)
    near_copy.start()
    shard_count, z_count, slot_dev, spread = shape
    query_count, qtok, dim = query_ref.shape
    cand_count = cand_ref.shape[1]
    width = pick_ref.shape[1]
    my_core = lax.rem(lax.div(where_ref[0], shard_count), 2)
    my_x = lax.rem(where_ref[0], 2)
    cand = cand_ref[...]
    cand = jnp.concatenate(
        [cand, jnp.zeros((query_count, width - cand_count), jnp.int32)], axis=1
    )
    tables = [
        jnp.broadcast_to(slot_ref[row : row + 1, :], (query_count, LANES))
        for row in range(slot_ref.shape[0])
    ]
    parts = []
    for part in range(width // LANES):
        ids = cand[:, part * LANES : (part + 1) * LANES]
        parts.append(lookup(tables, lax.div(ids, LANES), lax.rem(ids, LANES)))
    storage = jnp.concatenate(parts, axis=1)
    device = lax.div(storage, slot_dev)
    group = lax.div(device, shard_count)
    shard = lax.rem(device, shard_count)
    cell = lax.div(group, 2) * z_count + lax.div(shard, 2)
    code = (
        cell * SETS
        + jnp.bitwise_xor(lax.rem(group, 2), my_core) * 2
        + jnp.bitwise_xor(lax.rem(shard, 2), my_x)
    )
    pick_ref[...] = code * slot_dev + lax.rem(storage, slot_dev)
    lane = lax.broadcasted_iota(jnp.int32, (query_count, LANES), 1)
    named = jnp.zeros((query_count, LANES), jnp.float32)
    for visit in range(spread):
        first = visit * PER_VISIT
        hit = code[:, first : first + 1] == lane
        named = jnp.where(hit, 1.0, named)
    rows = query_count * qtok
    block_ref[0:rows, :] = query_ref[...].reshape(rows, dim)
    block_ref[rows : rows + query_count, :] = named.astype(jnp.bfloat16)
    near_copy.wait()


def prepare(where, queries, candidates, passage_slot, passages, shape):
    query_count, qtok, dim = queries.shape
    width = -(-candidates.shape[1] // LANES) * LANES
    vmem = pl.BlockSpec(memory_space=pltpu.VMEM)
    return pl.pallas_call(
        functools.partial(prepare_kernel, shape),
        out_shape=(
            jax.ShapeDtypeStruct((query_count * (qtok + 1), dim), jnp.bfloat16),
            jax.ShapeDtypeStruct((query_count, width), jnp.int32),
            jax.ShapeDtypeStruct(passages.shape, passages.dtype),
        ),
        in_specs=[
            pl.BlockSpec(memory_space=pltpu.SMEM),
            vmem,
            vmem,
            vmem,
            pl.BlockSpec(memory_space=pl.ANY),
        ],
        out_specs=(vmem, vmem, pl.BlockSpec(memory_space=pl.ANY)),
        scratch_shapes=[pltpu.SemaphoreType.DMA(())],
        compiler_params=pltpu.CompilerParams(vmem_limit_bytes=8 << 20),
        name="prepare",
    )(where, queries, candidates, passage_slot, passages)


def score_kernel(plan, *refs):
    source_count, base, set_ids, has_carry, qtok, y_count, z_count = plan
    where_ref = refs[0]
    arrays = refs[1 : 1 + source_count]
    stores = refs[1 + source_count : 1 + source_count + len(set_ids)]
    rest = refs[1 + source_count + len(set_ids) :]
    if has_carry:
        rest[1][...] = rest[0][...]
        rest = rest[1:]
    (out_ref, qs, ms, ps, mask_v, mask_s, todo, setof, best, copy_sem) = rest
    slots, ptok, dim = stores[0].shape
    rows = qs.shape[1]
    query_count = rows // qtok
    my_y = lax.div(where_ref[0], 4 * z_count)
    my_z = lax.rem(lax.div(where_ref[0], 2), z_count)
    me = my_y * z_count + my_z

    m_copies = [
        pltpu.make_async_copy(
            array.at[pl.ds(rows, query_count)], ms.at[position], copy_sem.at[3]
        )
        for position, array in enumerate(arrays)
    ]
    q_copies = [
        pltpu.make_async_copy(array.at[pl.ds(0, rows)], qs.at[position], copy_sem.at[0])
        for position, array in enumerate(arrays)
    ]
    p_copies = [
        pltpu.make_async_copy(store, ps.at[position], copy_sem.at[1])
        for position, store in enumerate(stores)
    ]
    for copy in m_copies + q_copies + p_copies:
        copy.start()
    for copy in m_copies:
        copy.wait()

    weight = lax.shift_left(1, lax.broadcasted_iota(jnp.int32, (query_count, LANES), 0))
    weight = weight.astype(jnp.float32)
    for position in range(source_count):
        named = ms[position].astype(jnp.float32)
        mask_v[position : position + 1, :] = jnp.sum(
            named * weight, axis=0, keepdims=True
        ).astype(jnp.int32)
    mask_copy = pltpu.make_async_copy(mask_v, mask_s, copy_sem.at[2])
    mask_copy.start()
    mask_copy.wait()

    total = jnp.int32(0)
    for position, set_id in enumerate(set_ids):
        start = total

        def one_source(source, filled, set_id=set_id):
            bits = mask_s[source, me * SETS + set_id]
            for query in range(query_count):
                todo[filled] = source * query_count + query
                filled = filled + (lax.shift_right_logical(bits, query) & 1)
            return filled

        filled = lax.fori_loop(0, source_count, one_source, start)
        last = todo[jnp.maximum(filled - 1, 0)]
        for extra in range(GROUP - 1):
            todo[filled + extra] = last
        total = lax.div(filled + (GROUP - 1), GROUP) * GROUP

        def mark(group, carry, position=position):
            setof[group] = position
            return carry

        lax.fori_loop(lax.div(start, GROUP), lax.div(total, GROUP), mark, 0)
    groups = lax.div(total, GROUP)

    for copy in q_copies + p_copies:
        copy.wait()

    columns = GROUP * qtok
    adder = jnp.where(
        lax.div(lax.broadcasted_iota(jnp.int32, (GROUP, columns), 1), qtok)
        == lax.broadcasted_iota(jnp.int32, (GROUP, columns), 0),
        1.0,
        0.0,
    ).astype(jnp.bfloat16)
    contract_last = (((1,), (1,)), ((), ()))
    quarter = lax.div(lax.broadcasted_iota(jnp.int32, (1, SETS * slots), 1), slots)

    def finish(group, slot):
        value = best[slot]
        high = value.astype(jnp.bfloat16)
        low = (value - high.astype(jnp.float32)).astype(jnp.bfloat16)
        score = lax.dot_general(adder, high, contract_last, preferred_element_type=jnp.float32)
        score += lax.dot_general(adder, low, contract_last, preferred_element_type=jnp.float32)
        score = score * (1.0 / qtok)
        score = jnp.concatenate([score] * SETS, axis=1)
        position = setof[group]
        set_id = jnp.int32(set_ids[0])
        for other in range(1, len(set_ids)):
            set_id = jnp.where(position == other, set_ids[other], set_id)
        for item in range(GROUP):
            entry = todo[group * GROUP + item]
            source = base + lax.div(entry, query_count)
            from_y = lax.rem(my_y - lax.div(source, z_count) + y_count, y_count)
            from_z = jnp.bitwise_xor(my_z, lax.rem(source, z_count))
            row = (from_y * z_count + from_z) * query_count + lax.rem(entry, query_count)
            out_ref[pl.ds(row, 1), :] = jnp.where(
                quarter == set_id, score[item : item + 1], out_ref[pl.ds(row, 1), :]
            )

    def search(group, slot):
        pieces = []
        for item in range(GROUP):
            entry = todo[group * GROUP + item]
            source = lax.div(entry, query_count)
            first = pl.multiple_of(lax.rem(entry, query_count) * qtok, qtok)
            pieces.append(qs[source, pl.ds(first, qtok), :])
        query = jnp.concatenate(pieces, axis=0)
        position = setof[group]
        step = 8
        for first in range(0, slots, step):
            tokens = ps[position, first : first + step].reshape(step * ptok, dim)
            similarity = lax.dot_general(
                tokens, query, contract_last, preferred_element_type=jnp.float32
            )
            similarity = similarity.reshape(step, ptok // 8, 8, columns)
            top = similarity[:, 0]
            for other in range(1, ptok // 8):
                top = jnp.maximum(top, similarity[:, other])
            best[slot, first : first + step, :] = jnp.max(top, axis=1)

    pairs = lax.div(groups, 2)
    odd = groups > 2 * pairs

    def search_pair(pair):
        search(2 * pair, 0)
        search(2 * pair + 1, 1)

    def finish_pair(pair):
        finish(2 * pair, 0)
        finish(2 * pair + 1, 1)

    @pl.when(pairs > 0)
    def _():
        search_pair(0)

        @pl.loop(1, pairs)
        def _(pair):
            finish_pair(pair - 1)
            search_pair(pair)

        @pl.when(odd)
        def _():
            finish_pair(pairs - 1)
            search(groups - 1, 0)
            finish(groups - 1, 0)

        @pl.when(jnp.logical_not(odd))
        def _():
            finish_pair(pairs - 1)

    @pl.when(groups == 1)
    def _():
        search(0, 0)
        finish(0, 0)


def score(where, arrays, base, stores, counts, qtok, carry):
    set_ids = tuple(stores)
    slots, ptok, dim = stores[set_ids[0]].shape
    block_rows = arrays[0].shape[0]
    query_count = block_rows // (qtok + 1)
    source_count = len(arrays)
    cells = counts[0] * counts[1]
    mask_rows = -(-source_count // 8) * 8
    entries = len(set_ids) * (source_count * query_count + GROUP) + 2 * GROUP
    plan = (source_count, base, set_ids, carry is not None, qtok, *counts)
    operands = [where, *arrays, *stores.values()]
    specs = [pl.BlockSpec(memory_space=pltpu.SMEM)]
    specs += [pl.BlockSpec(memory_space=pl.ANY)] * (source_count + len(set_ids))
    if carry is not None:
        operands.append(carry)
        specs.append(pl.BlockSpec(memory_space=pltpu.VMEM))
    work = source_count * query_count * len(set_ids) // 4
    return pl.pallas_call(
        functools.partial(score_kernel, plan),
        out_shape=jax.ShapeDtypeStruct((cells * query_count, SETS * slots), jnp.float32),
        in_specs=specs,
        out_specs=pl.BlockSpec(memory_space=pltpu.VMEM),
        scratch_shapes=[
            pltpu.VMEM((source_count, query_count * qtok, dim), jnp.bfloat16),
            pltpu.VMEM((source_count, query_count, dim), jnp.bfloat16),
            pltpu.VMEM((len(set_ids), slots, ptok, dim), jnp.bfloat16),
            pltpu.VMEM((mask_rows, LANES), jnp.int32),
            pltpu.SMEM((mask_rows, LANES), jnp.int32),
            pltpu.SMEM((entries,), jnp.int32),
            pltpu.SMEM((entries // GROUP + 1,), jnp.int32),
            pltpu.VMEM((2, slots, GROUP * qtok), jnp.float32),
            pltpu.SemaphoreType.DMA((4,)),
        ],
        compiler_params=pltpu.CompilerParams(vmem_limit_bytes=24 << 20),
        cost_estimate=pl.CostEstimate(
            flops=4 * work * slots * ptok * qtok * dim,
            bytes_accessed=source_count * block_rows * dim * 2
            + len(set_ids) * slots * ptok * dim * 2,
            transcendentals=0,
        ),
    )(*operands)


def select_kernel(scores_ref, pick_ref, out_ref):
    cells, _, wide = scores_ref.shape
    cand_count = out_ref.shape[1]
    tables = [
        scores_ref[cell, :, part * LANES : (part + 1) * LANES]
        for cell in range(cells)
        for part in range(wide // LANES)
    ]
    parts = []
    for part in range(pick_ref.shape[1] // LANES):
        pick = pick_ref[:, part * LANES : (part + 1) * LANES]
        parts.append(lookup(tables, lax.div(pick, LANES), lax.rem(pick, LANES)))
    out_ref[...] = jnp.concatenate(parts, axis=1)[:, :cand_count]


def select(scores, pick, cand_count):
    vmem = pl.BlockSpec(memory_space=pltpu.VMEM)
    return pl.pallas_call(
        select_kernel,
        out_shape=jax.ShapeDtypeStruct((pick.shape[0], cand_count), jnp.float32),
        in_specs=[vmem, vmem],
        out_specs=vmem,
        compiler_params=pltpu.CompilerParams(vmem_limit_bytes=8 << 20),
        name="select",
    )(scores, pick)


def local(mesh_shape, queries, passages, candidates, passage_slot):
    group_count, shard_count = mesh_shape
    y_count, z_count = group_count // 2, shard_count // 2
    cells = y_count * z_count
    query_count, qtok, _ = queries.shape
    slots = passages.shape[0]
    spread = candidates.shape[1] // PER_VISIT

    def index(yh, c, zh, x):
        return (yh * 2 + c) * shard_count + zh * 2 + x

    every = [
        (yh, c, zh, x)
        for yh in range(y_count)
        for c in range(2)
        for zh in range(z_count)
        for x in range(2)
    ]

    def move(value, to):
        pairs = [(index(*device), index(*to(*device))) for device in every]
        return lax.ppermute(value, AXES, pairs)

    group = lax.axis_index("group")
    shard = lax.axis_index("shard")
    where = (group * shard_count + shard).reshape(1).astype(jnp.int32)

    store_x = move(passages, lambda yh, c, zh, x: (yh, c, zh, 1 - x))
    store_c = move(passages, lambda yh, c, zh, x: (yh, 1 - c, zh, x))
    shape = (shard_count, z_count, slots, spread)
    fixed = [
        pltpu.with_memory_space_constraint(value, pltpu.HBM)
        for value in (queries, candidates, passage_slot.reshape(-1, LANES), passages)
    ]
    block, pick, store = prepare(where, *fixed, shape)
    line = [block] + [
        move(block, lambda yh, c, zh, x, kz=kz: (yh, c, zh ^ kz, x))
        for kz in range(1, z_count)
    ]
    beside = [
        move(part, lambda yh, c, zh, x, ky=ky: ((yh + ky) % y_count, c, zh, x))
        for ky in range(1, y_count)
        for part in line
    ]
    counts = (y_count, z_count)
    near = {0: store, 2: store_c}
    result = score(where, line[:2], 0, near, counts, qtok, None)
    result = score(where, line[2:], 2, near, counts, qtok, result)
    store_x, result = lax.optimization_barrier((store_x, result))
    store_xc = move(store_x, lambda yh, c, zh, x: (yh, 1 - c, zh, x))
    result = score(where, beside, z_count, near, counts, qtok, result)
    everything = score(
        where, line + beside, 0, {1: store_x, 3: store_xc}, counts, qtok, result
    )
    returned = everything.reshape(cells, query_count, SETS * slots)
    members = [
        [index(yh, c, zh, x) for yh in range(y_count) for zh in range(z_count)]
        for c in range(2)
        for x in range(2)
    ]
    returned = lax.all_to_all(
        returned, AXES, 0, 0, tiled=True, axis_index_groups=members
    )
    return select(returned, pick, candidates.shape[1])


def solution(mesh):
    mesh_shape = (mesh.shape["group"], mesh.shape["shard"])
    return jax.shard_map(
        functools.partial(local, mesh_shape),
        mesh=mesh,
        in_specs=(
            P(AXES, None, None),
            P(AXES, None, None),
            P(AXES, None),
            P(),
        ),
        out_specs=P(AXES, None),
        check_vma=False,
    )
```
